256 devices in a mesh: row: 64 (over z, y, core), col: 4 (over x).
Axes of the slice: x: 4, y: 4, z: 8, core: 2. Of those that a mesh axis runs over, the one named last changes fastest.
Arguments:
- rhs: float32 [7, 128, 64, 128], P(None, 'row'), may hold values from -6 to 6
- inv_diag: float32 [7, 128, 128, 128], P(None, 'row'), as said below
- lower_blocks: bfloat16 [6, 128, 16, 128, 128], P(None, 'row', 'col'), may hold values from -0.09375 to 0.09375
- col_index: int32 [6, 128, 16], P(None, 'row', 'col'), may hold values from 0 to 127, as said below
Outputs:
- solution: float32 [7, 128, 64, 128], P(None, 'row', 'col')
The draws below stay inside these ranges and needn't reach their ends.
Inputs may be any that keep to these rules, and one draw needn't show every extreme that they name: `col_index`: at level l (1 to 6) every entry lies below 2 ** l * 2. `inv_diag`: each block is lower triangular with a positive diagonal.
All inputs are finite; a program needn't handle non-finite values.
Results may differ from the reference program's by a relative error of at most 0.003.
Values may be sent and summed in bfloat16 or wider, within the bound.
A program may use at most 64 MiB of HBM per device.

```python
import math
import jax
import jax.numpy as jnp
from jax import lax

BLOCK = 128
RHS = 64
ROWS_LEV = 2
SLOTS = 16
UP = 6
LEVELS = 7
NROWS = 128


def draw_inv_diag(key, part):
    first, second = jax.random.split(key)
    shape = (LEVELS, NROWS, BLOCK, BLOCK)
    spread = jax.random.normal(first, shape, jnp.float32)
    spread = spread * (0.45 / math.sqrt(BLOCK))
    rows_at = lax.broadcasted_iota(jnp.int32, (BLOCK, BLOCK), 0)
    cols_at = lax.broadcasted_iota(jnp.int32, (BLOCK, BLOCK), 1)
    below = rows_at > cols_at
    middle = (rows_at == cols_at).astype(jnp.float32)
    scales = jax.random.uniform(second, (LEVELS, NROWS, BLOCK, 1), jnp.float32, 0.5, 1.5)
    return jnp.where(below, spread, 0.0) + middle * scales


def draw_col_index(key, part):
    limits = 2 ** (jnp.arange(UP, dtype=jnp.int32) + 1) * ROWS_LEV
    drawn = jax.random.randint(key, (UP, NROWS, SLOTS), 0, limits[:, None, None])
    drawn = drawn.at[UP - 1, 0, 0].set(NROWS - 1)
    drawn = drawn.at[0, 0, 1].set(0)
    return drawn.astype(jnp.int32)


def block_levels(stream_key, shape, pieces, smallest, largest):
    def one(position, shards_of):
        steps = jax.random.uniform(jax.random.fold_in(jax.random.fold_in(stream_key, 6), position), (shards_of,), jnp.float32, smallest / len(pieces), largest / len(pieces))
        return jnp.repeat(jnp.exp(steps), shape[position] // shards_of).reshape((-1,) + (1,) * (len(shape) - position - 1))

    loudness = one(*pieces[0])
    for cut in pieces[1:]:
        loudness = loudness * one(*cut)
    return loudness


def bell_draw(own_key, shape, scale, limit, cuts=(), held_as=jnp.bfloat16):
    result = jax.random.normal(own_key, shape, jnp.float32) * scale
    if len(cuts) > 0:
        result = block_levels(own_key, shape, cuts, -0.22, 0.18) * result
    return jnp.clip(result, min=-limit, max=limit).astype(held_as)


def setup_inputs(seed: int = 0) -> dict:
    key_of = jax.random.split(jax.random.key(seed), 5)
    return {
        "rhs": bell_draw(key_of[0], (LEVELS, NROWS, RHS, BLOCK), 1.0, 6.0, ((1, 64),), jnp.float32),
        "inv_diag": draw_inv_diag(jax.random.fold_in(key_of[4], 71), 0),
        "lower_blocks": bell_draw(key_of[2], (UP, NROWS, SLOTS, BLOCK, BLOCK), (2 * SLOTS * BLOCK) ** -0.5, 0.09375, ((1, 64), (2, 4))),
        "col_index": draw_col_index(jax.random.fold_in(key_of[4], 71), 0),
    }


def apply_inverse(resid, inverse):
    return jnp.einsum("nsq,nrq->nsr", resid, inverse, precision=lax.Precision.HIGHEST)


def reference(rhs, inv_diag, lower_blocks, col_index):
    total_rows = rhs.shape[1]
    results = [apply_inverse(rhs[0], inv_diag[0])]
    for level in range(1, UP + 1):
        rounded = results[-1].astype(jnp.bfloat16)
        group_rows = (2 ** level) * ROWS_LEV
        base = (jnp.arange(total_rows, dtype=jnp.int32) // group_rows) * group_rows
        update = jnp.zeros(rhs.shape[1:], jnp.float32)
        for slot in range(SLOTS):
            picked = rounded[base + col_index[level - 1, :, slot].astype(jnp.int32)]
            update = update + jnp.einsum("nsq,nrq->nsr", picked.astype(jnp.float32), lower_blocks[level - 1, :, slot].astype(jnp.float32))
        results.append(apply_inverse(rhs[level] - update, inv_diag[level]))
    return jnp.stack(results, 0)
```

```python
import functools

import jax
import jax.numpy as jnp
from jax import lax
from jax.experimental import pallas as pl
from jax.experimental.pallas import tpu as pltpu
from jax.sharding import PartitionSpec as P

MESH = pl.DeviceIdType.MESH
LOCAL_LEVELS = 3
SPLIT_ABOVE = 4
FEED = (0, 1, 1, 1, 1, 1, 2, 0, 4, 0, 4, 0)


def nt_dot(a, b, precision=None):
    return lax.dot_general(
        a, b, (((1,), (1,)), ((), ())), precision=precision, preferred_element_type=jnp.float32
    )


def inverse_dot(resid, inverse):
    return nt_dot(resid, inverse, lax.Precision.HIGHEST)


def kernel(depth, near, cols, rhs, inv, low, idx, out, *scratch):
    s = dict(zip(scratch_names(depth, near), scratch, strict=True))
    row, col = lax.axis_index("row"), lax.axis_index("col")
    share = rhs.shape[2] // cols
    slots = low.shape[2]
    far = depth - near
    core = row % 2
    mate = row + 1 - 2 * core
    rhs0, rhsq, invv, lowa, lows, idxv, idxs, idxo, pairs = (
        s[k] for k in ("rhs0", "rhsq", "invv", "lowa", "lows", "idxv", "idxs", "idxo", "pairs")
    )

    load = s["load_sem"]
    quarter = pl.ds(pl.multiple_of(col * share, share), share)
    load_rhs0 = pltpu.make_async_copy(rhs.at[0], rhs0, load.at[0])
    load_inv0 = pltpu.make_async_copy(inv.at[0], invv.at[0], load.at[1])
    load_idx = pltpu.make_async_copy(idx, idxv.at[col], load.at[2])
    load_own = pltpu.make_async_copy(idx, idxo, load.at[3])
    load_low = pltpu.make_async_copy(low.at[pl.ds(0, near)], lowa, load.at[4])
    load_inv = pltpu.make_async_copy(
        inv.at[pl.ds(1, depth)], invv.at[pl.ds(1, depth)], load.at[5]
    )
    load_rhs = pltpu.make_async_copy(
        rhs.at[pl.ds(1, depth), :, quarter], rhsq, load.at[6]
    )
    load_far = [
        pltpu.make_async_copy(low.at[near + i], lows.at[i, col], s["own_sem"].at[i])
        for i in range(far)
    ]
    for copy in (load_rhs0, load_inv0, load_idx, load_own, load_low, load_inv, load_rhs, *load_far):
        copy.start()

    barrier = pltpu.get_barrier_semaphore()
    greeted = 0

    def greet(target):
        pl.semaphore_signal(barrier, 1, device_id=target, device_id_type=MESH)

    for bit in reversed(range(1, depth)):
        n = 2 << bit
        greet((row - row % n + (row % n + n // 2) % n, col))
        greeted += 1
    for e in (2, 1, 3, 0):
        greet((mate, (col + e) % cols))
        greeted += 1
        if e:
            greet((row, (col + e) % cols))
            greeted += 1

    load_rhs0.wait()
    load_inv0.wait()
    for n in range(2):
        x0 = inverse_dot(rhs0[n], invv[0, n])
        pairs[core * 2 + n] = x0.astype(jnp.bfloat16)
        rhs0[n] = x0
    pl.semaphore_wait(barrier, greeted)

    def send(src, dst, send_sem, recv_sem, target):
        pltpu.make_async_remote_copy(
            src_ref=src, dst_ref=dst, send_sem=send_sem, recv_sem=recv_sem,
            device_id=target, device_id_type=MESH,
        ).start()

    def wait_bytes(ref, sem):
        pltpu.make_async_copy(ref, ref, sem).wait()

    pieces = [(i, n, half) for i in range(far) for n in range(2) for half in range(2)]

    def feed(count):
        for i, n, half in pieces[:count]:
            at = pl.ds(half * (slots // 2), slots // 2)
            for e in (2, 1, 3):
                send(low.at[near + i, n, at], lows.at[i, col, n, at],
                     s["low_send"].at[i], s["low_recv"].at[i], (row, (col + e) % cols))
        del pieces[:count]

    mine = pairs.at[pl.ds(core * 2, 2)]
    send(mine, mine, s["gather_send"].at[0], s["gather_recv"].at[0], (mate, col))
    load_idx.wait()
    for e in (2, 1, 3):
        send(idxv.at[col], idxv.at[col], s["idx_send"], s["idx_recv"], (row, (col + e) % cols))
    feed(FEED[0])
    for n in range(2):
        out[0, n] = rhs0[n, quarter]
    load_own.wait()
    load_low.wait()
    load_inv.wait()
    load_rhs.wait()

    for level in range(1, depth + 1):
        n_rows = 1 << level
        gather = pairs if level == 1 else s[f"gather{level}"]
        recv = s["gather_recv"].at[level - 1]
        split = is_split(level, near)
        if level == 1:
            wait_bytes(gather.at[pl.ds(0, 2)], recv)
        elif level <= near:
            flat = gather.reshape(cols * 2 * n_rows, share, gather.shape[-1])
            wait_bytes(flat.at[pl.ds(0, 2 * (n_rows * cols - 1))], recv)
        elif split:
            wait_bytes(gather.at[0, pl.ds(0, n_rows // 2 - 1)], recv)
            half = gather.at[core]
            sems = s["mate_send"].at[level - 1], s["mate_recv"].at[level - 1]
            send(half, half, *sems, (mate, col))
        else:
            wait_bytes(gather.at[pl.ds(0, 2 * (n_rows - 1))], recv)
        if level <= near:
            part, got = s["part"], s["got"]
            for n in range(2):
                picked, blocks = [], []
                for k in range(slots):
                    at = idxo[n, k, level - 1]
                    one = gather[at] if level == 1 else gather[:, at].reshape(cols * share, -1)
                    picked.append(one)
                    blocks.append(lowa[level - 1, n, k])
                partial = nt_dot(jnp.concatenate(picked, 1), jnp.concatenate(blocks, 1))
                part[level - 1, :, n] = partial.reshape(cols, share, -1)
            for e in (2, 1, 3):
                to = (col + e) % cols
                send(part.at[level - 1, to], got.at[level - 1, e - 1], s["part_send"].at[level - 1],
                     s["part_recv"].at[level - 1], (row, to))
            feed(FEED[2 * level - 1])
            wait_bytes(got.at[level - 1], s["part_recv"].at[level - 1])
            total = (part[level - 1, col] + got[level - 1, 0]) + (got[level - 1, 1] + got[level - 1, 2])
        else:
            i = level - near - 1
            if i == 0:
                wait_bytes(idxv.at[pl.ds(0, cols - 1)], s["idx_recv"])
                to_scalar = pltpu.make_async_copy(idxv, idxs, load.at[7])
                to_scalar.start()
                to_scalar.wait()
            load_far[i].wait()
            wait_bytes(lows.at[i, pl.ds(0, cols - 1)], s["low_recv"].at[i])
            if split:
                wait_bytes(gather.at[0], s["mate_recv"].at[level - 1])
            sums = []
            for n in range(2):
                picked, blocks = [], []
                for e in range(cols):
                    for k in range(slots):
                        at = idxs[e, n, k, level - 1]
                        picked.append(gather[(at >> 1) & 1, at >> 2, at & 1] if split else gather[at])
                        blocks.append(lows[i, e, n, k])
                sums.append(nt_dot(jnp.concatenate(picked, 1), jnp.concatenate(blocks, 1)))
            total = jnp.stack(sums, 0)
        x = [inverse_dot(rhsq[level - 1, n] - total[n], invv[level, n]) for n in range(2)]
        if level < depth:
            later = 2 * n_rows
            base, here = row - row % later, row % later
            onward = s[f"gather{level + 1}"]
            sems = s["gather_send"].at[level], s["gather_recv"].at[level]
            if level < near:
                mine = onward.at[col, pl.ds(2 * here, 2)]

                def to_rows(d, _):
                    for e in (2, 1, 3, 0):
                        send(mine, mine, *sems, (base + (here + d) % later, (col + e) % cols))
                    return _

            elif is_split(level + 1, near):
                mine = onward.at[core, here // 2]

                def to_rows(d, _):
                    chip = (here // 2 + d) % (later // 2)
                    send(mine, mine, *sems, (base + chip * 2 + core, col))
                    return _

            else:
                mine = onward.at[pl.ds(2 * here, 2)]

                def to_rows(d, _):
                    send(mine, mine, *sems, (base + (here + d) % later, col))
                    return _

            for n in range(2):
                mine[n] = x[n].astype(jnp.bfloat16)
            if level < near:
                for e in (2, 1, 3):
                    send(mine, mine, *sems, (row, (col + e) % cols))
            lax.fori_loop(1, later // 2 if is_split(level + 1, near) else later, to_rows, 0)
            due = sum(i < level + 1 - near for i, _, _ in pieces)
            feed(max(FEED[2 * level], due))
        for n in range(2):
            out[level, n] = x[n]

    wait_bytes(idxv.at[pl.ds(0, cols - 1)], s["idx_send"])
    wait_bytes(pairs.at[pl.ds(0, 2)], s["gather_send"].at[0])
    for level in range(1, depth + 1):
        gather = None if level == 1 else s[f"gather{level}"]
        sent = s["gather_send"].at[level - 1]
        if 1 < level <= near:
            flat = gather.reshape(cols * (2 << level), share, gather.shape[-1])
            wait_bytes(flat.at[pl.ds(0, 2 * ((cols << level) - 1))], sent)
        elif is_split(level, near):
            wait_bytes(gather.at[0, pl.ds(0, (1 << level) // 2 - 1)], sent)
            wait_bytes(gather.at[0], s["mate_send"].at[level - 1])
        elif level > near:
            wait_bytes(gather.at[pl.ds(0, 2 * ((1 << level) - 1))], sent)
        if level <= near:
            wait_bytes(s["got"].at[level - 1], s["part_send"].at[level - 1])
        else:
            wait_bytes(lows.at[level - near - 1, pl.ds(0, cols - 1)], s["low_send"].at[level - near - 1])


def is_split(level, near):
    return level > max(near, SPLIT_ABOVE)


NAMES = (
    "rhs0", "rhsq", "invv", "lowa", "lows", "idxv", "idxs", "idxo", "pairs", "part", "got",
    "load_sem", "own_sem", "idx_send", "idx_recv", "gather_send", "gather_recv",
    "part_send", "part_recv", "low_send", "low_recv", "mate_send", "mate_recv",
)


def scratch_names(depth, near):
    return [*NAMES, *(f"gather{level}" for level in range(2, depth + 1))]


def on_device(depth, near, cols, rhs, inv, low, idx):
    levels, two, wide, block = rhs.shape
    share = wide // cols
    slots = low.shape[2]
    far = depth - near
    idx = idx.transpose(1, 2, 0)
    dma = pltpu.SemaphoreType.DMA
    f32, bf16 = jnp.float32, jnp.bfloat16
    scratch = [
        pltpu.VMEM((two, wide, block), f32),
        pltpu.VMEM((depth, two, share, block), f32),
        pltpu.VMEM((levels, two, block, block), f32),
        pltpu.VMEM((near, two, slots, block, block), bf16),
        pltpu.VMEM((far, cols, two, slots, block, block), bf16),
        pltpu.VMEM((cols, *idx.shape), jnp.int32),
        pltpu.SMEM((cols, *idx.shape), jnp.int32),
        pltpu.SMEM(idx.shape, jnp.int32),
        pltpu.VMEM((2 * two, wide, block), bf16),
        pltpu.VMEM((near, cols, two, share, block), f32),
        pltpu.VMEM((near, cols - 1, two, share, block), f32),
        dma((8,)), dma((far,)), dma, dma,
        dma((depth,)), dma((depth,)), dma((near,)), dma((near,)), dma((far,)), dma((far,)),
        dma((depth,)), dma((depth,)),
    ]
    for level in range(2, depth + 1):
        rows = two << level
        lead = (cols, rows) if level <= near else (2, rows // 4, 2) if is_split(level, near) else (rows,)
        scratch.append(pltpu.VMEM((*lead, share, block), bf16))
    stay = pl.BlockSpec(memory_space=pltpu.HBM)
    return pl.pallas_call(
        functools.partial(kernel, depth, near, cols),
        out_shape=jax.ShapeDtypeStruct((levels, two, share, block), f32),
        in_specs=[stay] * 4,
        out_specs=pl.BlockSpec(memory_space=pltpu.VMEM),
        scratch_shapes=scratch,
        compiler_params=pltpu.CompilerParams(
            collective_id=0, has_side_effects=True, vmem_limit_bytes=61 << 20
        ),
    )(rhs, inv, low, idx)


def solution(mesh):
    depth = mesh.shape["row"].bit_length() - 1
    near = min(LOCAL_LEVELS, depth - 1)
    return jax.shard_map(
        functools.partial(on_device, depth, near, mesh.shape["col"]),
        mesh=mesh,
        in_specs=(
            P(None, "row", None, None),
            P(None, "row", None, None),
            P(None, "row", "col", None, None),
            P(None, "row", "col"),
        ),
        out_specs=P(None, "row", "col", None),
        check_vma=False,
    )
```

```python
import functools

import jax
import jax.numpy as jnp
from jax import lax
from jax.experimental import pallas as pl
from jax.experimental.pallas import tpu as pltpu
from jax.sharding import PartitionSpec as P

MESH = pl.DeviceIdType.MESH
ROW_LEVELS = 3
SPLIT_ABOVE = 4
FEED = (0, 0, 2, 2, 2, 3, 3)


def nt_dot(a, b, precision=None):
    return lax.dot_general(
        a, b, (((1,), (1,)), ((), ())), precision=precision, preferred_element_type=jnp.float32
    )


def inverse_dot(resid, inverse):
    return nt_dot(resid, inverse, lax.Precision.HIGHEST)


def kernel(depth, mid, cols, rhs, inv, low, idx, out, *scratch):
    s = dict(zip(scratch_names(depth), scratch, strict=True))
    row, col = lax.axis_index("row"), lax.axis_index("col")
    share = rhs.shape[2] // cols
    slots = low.shape[2]
    far, chips = depth - mid, mid - 1
    core, chip = row % 2, row // 2
    mate = row + 1 - 2 * core
    home, place = col // 2, col % 2
    at_home = core == home
    rhs0, rhsq, invv, lowa, lows, lowc, idxv, idxs, idxo, pairs = (
        s[k]
        for k in ("rhs0", "rhsq", "invv", "lowa", "lows", "lowc", "idxv", "idxs", "idxo", "pairs")
    )

    def send(src, dst, send_sem, recv_sem, target):
        pltpu.make_async_remote_copy(
            src_ref=src, dst_ref=dst, send_sem=send_sem, recv_sem=recv_sem,
            device_id=target, device_id_type=MESH,
        ).start()

    def hand(here, src, dst, send_sem, recv_sem, target):
        @pl.when(here)
        def _():
            pltpu.make_async_copy(src, dst, recv_sem).start()

        @pl.when(jnp.logical_not(here))
        def _():
            send(src, dst, send_sem, recv_sem, target)

    def wait_bytes(ref, sem):
        pltpu.make_async_copy(ref, ref, sem).wait()

    def wait_if_away(ref, sem):
        @pl.when(jnp.logical_not(at_home))
        def _():
            wait_bytes(ref, sem)

    load = s["load_sem"]
    quarter = pl.ds(pl.multiple_of(col * share, share), share)
    load_rhs0 = pltpu.make_async_copy(rhs.at[0], rhs0, load.at[0])
    load_inv0 = pltpu.make_async_copy(inv.at[0], invv.at[0], load.at[1])
    load_idx = pltpu.make_async_copy(idx, idxv.at[core, col], load.at[2])
    load_own = pltpu.make_async_copy(idx, idxo, load.at[3])
    load_low = pltpu.make_async_copy(low.at[0], lowa, load.at[4])
    load_inv = pltpu.make_async_copy(
        inv.at[pl.ds(1, depth)], invv.at[pl.ds(1, depth)], load.at[5]
    )
    load_rhs = pltpu.make_async_copy(
        rhs.at[pl.ds(1, depth), :, quarter], rhsq, load.at[6]
    )
    load_far = [
        pltpu.make_async_copy(low.at[mid + i], lows.at[i, col], s["own_sem"].at[i])
        for i in range(far)
    ]
    for copy in (load_rhs0, load_inv0, load_idx, load_own, load_low, load_inv, load_rhs, *load_far):
        copy.start()

    barrier = pltpu.get_barrier_semaphore()
    greeted = 0

    def greet(target):
        pl.semaphore_signal(barrier, 1, device_id=target, device_id_type=MESH)

    for bit in reversed(range(1, depth)):
        n = 2 << bit
        greet((row - row % n + (row % n + n // 2) % n, col))
        greeted += 1
    for e in (2, 1, 3, 0):
        greet((mate, (col + e) % cols))
        greeted += 1
        if e:
            greet((row, (col + e) % cols))
            greeted += 1

    load_rhs0.wait()
    load_inv0.wait()
    for n in range(2):
        x0 = inverse_dot(rhs0[n], invv[0, n])
        pairs[core * 2 + n] = x0.astype(jnp.bfloat16)
        rhs0[n] = x0
    pl.semaphore_wait(barrier, greeted)

    mine = pairs.at[pl.ds(core * 2, 2)]
    send(mine, mine, s["gather_send"].at[0], s["gather_recv"].at[0], (mate, col))

    def feed_row(j):
        for n in range(2):
            to = core * 2 + n
            for t in range(2):
                at = pl.ds(t * (slots // 2), slots // 2)
                hand((to == col) & (core == t), low.at[j + 1, n, at], lowc.at[j, col, at],
                     s["row_send"].at[j], s["row_recv"].at[j], (chip * 2 + t, to))

    pieces = [(i, n, half) for i in range(far) for n in range(2) for half in range(2)]

    def feed(count):
        for i, n, half in pieces[:count]:
            at = pl.ds(half * (slots // 2), slots // 2)
            for e in (2, 1, 3):
                send(low.at[mid + i, n, at], lows.at[i, col, n, at],
                     s["low_send"].at[i], s["low_recv"].at[i], (row, (col + e) % cols))
        del pieces[:count]

    feed_row(0)
    load_idx.wait()
    for e in (2, 1, 3, 0):
        for target in (row, mate):
            if e or target is mate:
                send(idxv.at[core, col], idxv.at[core, col], s["idx_send"], s["idx_recv"],
                     (target, (col + e) % cols))

    @pl.when(at_home)
    def _():
        for j in range(chips):
            for target, half in ((row, core), (mate, 1 - core)):
                at = pl.ds(pl.multiple_of(half * 2 * share, 2 * share), 2 * share)
                for src, dst, k in (
                    (rhs.at[j + 2, place, at], s["rhsc"].at[j], 0),
                    (inv.at[j + 2, place], s["invc"].at[j], 1),
                ):
                    if target is row:
                        pltpu.make_async_copy(src, dst, s["side_recv"].at[j, k]).start()
                    else:
                        send(src, dst, s["side_send"].at[j, k], s["side_recv"].at[j, k], (mate, col))

    feed(FEED[0])
    for n in range(2):
        out[0, n] = rhs0[n, quarter]
    load_own.wait()
    load_low.wait()
    load_inv.wait()
    load_rhs.wait()

    for level in range(1, depth + 1):
        n_rows = 1 << level
        gather = pairs if level == 1 else s[f"gather{level}"]
        recv = s["gather_recv"].at[level - 1]
        split = is_split(level, mid)
        if level == 1:
            wait_bytes(gather.at[pl.ds(0, 2)], recv)
        elif level <= mid + 1:
            wait_bytes(gather, recv)
        elif split:
            wait_bytes(gather.at[0, pl.ds(0, n_rows // 2 - 1)], recv)
            half = gather.at[core]
            sems = s["mate_send"].at[level - 1], s["mate_recv"].at[level - 1]
            send(half, half, *sems, (mate, col))
        else:
            wait_bytes(gather.at[pl.ds(0, 2 * (n_rows - 1))], recv)
        if level == 1:
            part, got = s["part"], s["got"]
            for n in range(2):
                picked, blocks = [], []
                for k in range(slots):
                    picked.append(gather[idxo[n, k, 0]])
                    blocks.append(lowa[n, k])
                partial = nt_dot(jnp.concatenate(picked, 1), jnp.concatenate(blocks, 1))
                part[:, n] = partial.reshape(cols, share, -1)
            for e in (2, 1, 3):
                to = (col + e) % cols
                send(part.at[to], got.at[e - 1], s["part_send"], s["part_recv"], (row, to))
            for j in range(1, chips):
                feed_row(j)
            feed(FEED[1])
            wait_bytes(idxv.reshape(2 * cols, *idx.shape).at[pl.ds(0, 2 * cols - 1)], s["idx_recv"])
            to_scalar = pltpu.make_async_copy(idxv, idxs, load.at[7])
            to_scalar.start()
            wait_bytes(got, s["part_recv"])
            total = (part[col] + got[0]) + (got[1] + got[2])
        elif level <= mid:
            j = level - 2
            wait_bytes(s["rhsc"].at[j], s["side_recv"].at[j, 0])
            wait_bytes(s["invc"].at[j], s["side_recv"].at[j, 1])
            wait_bytes(lowc.at[j, :, pl.ds(0, slots // 2)], s["pass_recv"].at[j])
            picked, blocks = [], []
            for e in range(cols):
                for k in range(slots):
                    at = idxs[home, e, place, k, level - 1]
                    picked.append(gather[at].reshape(2 * share, -1))
                    blocks.append(lowc[j, e, k])
            total = nt_dot(jnp.concatenate(picked, 1), jnp.concatenate(blocks, 1))
        else:
            i = level - mid - 1
            load_far[i].wait()
            wait_bytes(lows.at[i, pl.ds(0, cols - 1)], s["low_recv"].at[i])
            if split:
                wait_bytes(gather.at[0], s["mate_recv"].at[level - 1])
            sums = []
            for n in range(2):
                picked, blocks = [], []
                for e in range(cols):
                    for k in range(slots):
                        at = idxs[core, e, n, k, level - 1]
                        picked.append(gather[(at >> 1) & 1, at >> 2, at & 1] if split else gather[at])
                        blocks.append(lows[i, e, n, k])
                sums.append(nt_dot(jnp.concatenate(picked, 1), jnp.concatenate(blocks, 1)))
            total = jnp.stack(sums, 0)
        in_row = 1 < level <= mid
        if in_row:
            x = inverse_dot(s["rhsc"][level - 2] - total, s["invc"][level - 2])
            x = [x[q * share : (q + 1) * share] for q in range(2)]
        else:
            x = [inverse_dot(rhsq[level - 1, n] - total[n], invv[level, n]) for n in range(2)]
        if level < depth:
            later = 2 * n_rows
            base, here = row - row % later, row % later
            here_chip = here // 2
            onward = s[f"gather{level + 1}"]
            sems = s["gather_send"].at[level], s["gather_recv"].at[level]
            count = later // 2
            if level <= mid:
                mine = s["held"].at[level - 1]
                for n in range(2):
                    mine[n] = x[n].astype(jnp.bfloat16)
            if level == 1:
                slot = onward.at[pl.ds(here_chip * 4 + core * 2, 2), place]

                def to_chips(d, _):
                    target = base + (here_chip + d) % count * 2 + home
                    for e in (2, 1, 3, 0):
                        send(mine, slot, *sems, (target, (col + e) % cols))
                    return _

                for e in (2, 1, 3):
                    send(mine, slot, *sems, (chip * 2 + home, (col + e) % cols))
                hand(at_home, mine, slot, *sems, (mate, col))
            elif level < mid:
                slot = onward.at[here_chip * 4 + col]

                def to_chips(d, _):
                    target = base + (here_chip + d) % count * 2 + core
                    for e in (2, 1, 3, 0):
                        send(mine, slot, *sems, (target, (col + e) % cols))
                    return _

                for e in (2, 1, 3):
                    send(mine, slot, *sems, (row, (col + e) % cols))
                pltpu.make_async_copy(mine, slot, sems[1]).start()
            elif level == mid:
                slot = onward.at[here_chip * 4 + col]

                def to_chips(d, _):
                    target = base + (here_chip + d) % count * 2
                    for t in range(2):
                        for q in range(2):
                            send(mine.at[q], slot, *sems, (target + t, core * 2 + q))
                    return _

                for q in range(2):
                    to = core * 2 + q
                    send(mine.at[q], slot, *sems, (mate, to))
                    hand(to == col, mine.at[q], slot, *sems, (row, to))
            elif is_split(level + 1, mid):
                mine = onward.at[core, here_chip]

                def to_chips(d, _):
                    send(mine, mine, *sems, (base + (here_chip + d) % count * 2 + core, col))
                    return _

            else:
                mine = onward.at[pl.ds(2 * here, 2)]
                count = later

                def to_chips(d, _):
                    send(mine, mine, *sems, (base + (here + d) % later, col))
                    return _

            if level > mid:
                for n in range(2):
                    mine[n] = x[n].astype(jnp.bfloat16)
            lax.fori_loop(1, count, to_chips, 0)
            if level == 1:
                to_scalar.wait()
            if level < mid:
                j = level - 1
                half = pl.ds(core * (slots // 2), slots // 2)
                wait_bytes(lowc.at[j, :, pl.ds(0, slots // 2)], s["row_recv"].at[j])
                send(lowc.at[j, :, half], lowc.at[j, :, half], s["pass_send"].at[j], s["pass_recv"].at[j],
                     (mate, col))
            due = sum(i < level + 1 - mid for i, _, _ in pieces)
            feed(max(FEED[level + 1], due))
        if in_row:
            j = level - 2
            for q in range(2):
                s["wide"][j, q] = x[q]
                to = core * 2 + q
                hand((to == col) & at_home, s["wide"].at[j, q], s["owned"].at[j, place],
                     s["own_send"].at[j], s["own_recv"].at[j], (chip * 2 + home, to))
        else:
            for n in range(2):
                out[level, n] = x[n]

    for j in range(chips):
        wait_bytes(s["owned"].at[j], s["own_recv"].at[j])
        out[j + 2] = s["owned"][j]

    wait_bytes(idxv.reshape(2 * cols, *idx.shape).at[pl.ds(0, 2 * cols - 1)], s["idx_send"])
    wait_bytes(pairs.at[pl.ds(0, 2)], s["gather_send"].at[0])
    wait_bytes(s["got"], s["part_send"])
    for j in range(chips):
        wait_bytes(lowc.at[j, pl.ds(0, cols - 1), pl.ds(0, slots // 2)], s["row_send"].at[j])
        wait_if_away(lowc.at[j, 0, pl.ds(0, slots // 2)], s["row_send"].at[j])
        wait_bytes(lowc.at[j, :, pl.ds(0, slots // 2)], s["pass_send"].at[j])
        wait_bytes(s["wide"].at[j, 0], s["own_send"].at[j])
        wait_if_away(s["wide"].at[j, 0], s["own_send"].at[j])

    @pl.when(at_home)
    def _():
        for j in range(chips):
            wait_bytes(s["rhsc"].at[j], s["side_send"].at[j, 0])
            wait_bytes(s["invc"].at[j], s["side_send"].at[j, 1])

    for level in range(2, depth + 1):
        gather, sent = s[f"gather{level}"], s["gather_send"].at[level - 1]
        n_rows = 1 << level
        if level == 2 or level == mid + 1:
            one = gather.at[pl.ds(0, 2), 0] if level == 2 else gather.at[0]
            rest = gather.at[pl.ds(0, 7)] if level == 2 else gather.at[pl.ds(0, 2 * n_rows - 1)]
            wait_bytes(rest, sent)
            wait_if_away(one, sent)
        elif level <= mid:
            wait_bytes(gather.at[pl.ds(0, 2 * n_rows - 1)], sent)
        elif is_split(level, mid):
            wait_bytes(gather.at[0, pl.ds(0, n_rows // 2 - 1)], sent)
            wait_bytes(gather.at[0], s["mate_send"].at[level - 1])
        else:
            wait_bytes(gather.at[pl.ds(0, 2 * (n_rows - 1))], sent)
    for i in range(far):
        wait_bytes(lows.at[i, pl.ds(0, cols - 1)], s["low_send"].at[i])


def is_split(level, mid):
    return level > max(mid + 1, SPLIT_ABOVE)


NAMES = (
    "rhs0", "rhsq", "invv", "lowa", "lows", "lowc", "idxv", "idxs", "idxo", "pairs", "part", "got",
    "rhsc", "invc", "held", "wide", "owned", "load_sem", "own_sem", "idx_send", "idx_recv",
    "gather_send", "gather_recv", "part_send", "part_recv", "low_send", "low_recv", "mate_send",
    "mate_recv", "row_send", "row_recv", "pass_send", "pass_recv", "side_send", "side_recv",
    "own_send", "own_recv",
)


def scratch_names(depth):
    return [*NAMES, *(f"gather{level}" for level in range(2, depth + 1))]


def on_device(depth, mid, cols, rhs, inv, low, idx):
    levels, two, wide, block = rhs.shape
    share = wide // cols
    slots = low.shape[2]
    far, chips = depth - mid, mid - 1
    idx = idx.transpose(1, 2, 0)
    dma = pltpu.SemaphoreType.DMA
    f32, bf16 = jnp.float32, jnp.bfloat16
    scratch = [
        pltpu.VMEM((two, wide, block), f32),
        pltpu.VMEM((depth, two, share, block), f32),
        pltpu.VMEM((levels, two, block, block), f32),
        pltpu.VMEM((two, slots, block, block), bf16),
        pltpu.VMEM((far, cols, two, slots, block, block), bf16),
        pltpu.VMEM((chips, cols, slots, block, block), bf16),
        pltpu.VMEM((2, cols, *idx.shape), jnp.int32),
        pltpu.SMEM((2, cols, *idx.shape), jnp.int32),
        pltpu.SMEM(idx.shape, jnp.int32),
        pltpu.VMEM((2 * two, wide, block), bf16),
        pltpu.VMEM((cols, two, share, block), f32),
        pltpu.VMEM((cols - 1, two, share, block), f32),
        pltpu.VMEM((chips, 2 * share, block), f32),
        pltpu.VMEM((chips, block, block), f32),
        pltpu.VMEM((mid, 2, share, block), bf16),
        pltpu.VMEM((chips, 2, share, block), f32),
        pltpu.VMEM((chips, two, share, block), f32),
        dma((8,)), dma((far,)), dma, dma,
        dma((depth,)), dma((depth,)), dma, dma, dma((far,)), dma((far,)), dma((depth,)),
        dma((depth,)), dma((chips,)), dma((chips,)), dma((chips,)), dma((chips,)), dma((chips, 2)), dma((chips, 2)),
        dma((chips,)), dma((chips,)),
    ]
    for level in range(2, depth + 1):
        rows = two << level
        lead = (rows, 2) if level <= mid else (2, rows // 4, 2) if is_split(level, mid) else (rows,)
        scratch.append(pltpu.VMEM((*lead, share, block), bf16))
    stay = pl.BlockSpec(memory_space=pltpu.HBM)
    return pl.pallas_call(
        functools.partial(kernel, depth, mid, cols),
        out_shape=jax.ShapeDtypeStruct((levels, two, share, block), f32),
        in_specs=[stay] * 4,
        out_specs=pl.BlockSpec(memory_space=pltpu.VMEM),
        scratch_shapes=scratch,
        compiler_params=pltpu.CompilerParams(
            collective_id=0, has_side_effects=True, vmem_limit_bytes=61 << 20
        ),
    )(rhs, inv, low, idx)


def solution(mesh):
    depth = mesh.shape["row"].bit_length() - 1
    mid = min(ROW_LEVELS, depth - 1)
    return jax.shard_map(
        functools.partial(on_device, depth, mid, mesh.shape["col"]),
        mesh=mesh,
        in_specs=(
            P(None, "row", None, None),
            P(None, "row", None, None),
            P(None, "row", "col", None, None),
            P(None, "row", "col"),
        ),
        out_specs=P(None, "row", "col", None),
        check_vma=False,
    )
```

```python
import functools

import jax
import jax.numpy as jnp
from jax import lax
from jax.experimental import pallas as pl
from jax.experimental.pallas import tpu as pltpu
from jax.sharding import PartitionSpec as P

MESH = pl.DeviceIdType.MESH
ROW_LEVELS = 3
SPLIT_ABOVE = 4
FEED = (0, 0, 6, 4, 6, 8, 0)


def nt_dot(a, b, precision=None):
    return lax.dot_general(
        a, b, (((1,), (1,)), ((), ())), precision=precision, preferred_element_type=jnp.float32
    )


PREC = lax.Precision.HIGH


def inverse_dot(resid, inverse):
    return nt_dot(resid, inverse, PREC)


def kernel(depth, mid, cols, rhs, inv, low, idx, out, *scratch):
    s = dict(zip(scratch_names(depth), scratch, strict=True))
    row, col = lax.axis_index("row"), lax.axis_index("col")
    share = rhs.shape[2] // cols
    slots = low.shape[2]
    far, chips = depth - mid, mid - 1
    core, chip = row % 2, row // 2
    mate = row + 1 - 2 * core
    home, place = col // 2, col % 2
    at_home = core == home
    rhs0, rhsq, invv, lowa, lows, lowc, idxv, idxs, idxo, pairs = (
        s[k]
        for k in ("rhs0", "rhsq", "invv", "lowa", "lows", "lowc", "idxv", "idxs", "idxo", "pairs")
    )

    def send(src, dst, send_sem, recv_sem, target):
        pltpu.make_async_remote_copy(
            src_ref=src, dst_ref=dst, send_sem=send_sem, recv_sem=recv_sem,
            device_id=target, device_id_type=MESH,
        ).start()

    def hand(here, src, dst, send_sem, recv_sem, target):
        @pl.when(here)
        def _():
            pltpu.make_async_copy(src, dst, recv_sem).start()

        @pl.when(jnp.logical_not(here))
        def _():
            send(src, dst, send_sem, recv_sem, target)

    def wait_bytes(ref, sem):
        pltpu.make_async_copy(ref, ref, sem).wait()

    def wait_if_away(ref, sem):
        @pl.when(jnp.logical_not(at_home))
        def _():
            wait_bytes(ref, sem)

    load = s["load_sem"]
    quarter = pl.ds(pl.multiple_of(col * share, share), share)
    load_rhs0 = pltpu.make_async_copy(rhs.at[0], rhs0, load.at[0])
    load_inv0 = pltpu.make_async_copy(inv.at[0], invv.at[0], load.at[1])
    load_idx = pltpu.make_async_copy(idx, idxv.at[core, col], load.at[2])
    load_own = pltpu.make_async_copy(idx, idxo, load.at[3])
    load_low = pltpu.make_async_copy(low.at[0], lowa, load.at[4])
    load_inv = pltpu.make_async_copy(
        inv.at[pl.ds(1, depth)], invv.at[pl.ds(1, depth)], load.at[5]
    )
    load_rhs = pltpu.make_async_copy(
        rhs.at[pl.ds(1, depth), :, quarter], rhsq, load.at[6]
    )
    load_far = [
        pltpu.make_async_copy(low.at[mid + i], lows.at[i, col], s["own_sem"].at[i])
        for i in range(far)
    ]
    for copy in (load_rhs0, load_inv0, load_idx, load_own, load_low, load_inv, load_rhs, *load_far):
        copy.start()

    barrier = pltpu.get_barrier_semaphore()
    greeted = 0

    def greet(target):
        pl.semaphore_signal(barrier, 1, device_id=target, device_id_type=MESH)

    for bit in reversed(range(1, depth)):
        n = 2 << bit
        greet((row - row % n + (row % n + n // 2) % n, col))
        greeted += 1
    for e in (2, 1, 3, 0):
        greet((mate, (col + e) % cols))
        greeted += 1
        if e:
            greet((row, (col + e) % cols))
            greeted += 1

    load_rhs0.wait()
    load_inv0.wait()
    for n in range(2):
        x0 = inverse_dot(rhs0[n], invv[0, n])
        pairs[core * 2 + n] = x0.astype(jnp.bfloat16)
        rhs0[n] = x0
    pl.semaphore_wait(barrier, greeted)

    mine = pairs.at[pl.ds(core * 2, 2)]
    send(mine, mine, s["gather_send"].at[0], s["gather_recv"].at[0], (mate, col))

    def feed_row(j):
        for n in range(2):
            to = core * 2 + n
            for t in range(2):
                at = pl.ds(t * (slots // 2), slots // 2)
                hand((to == col) & (core == t), low.at[j + 1, n, at], lowc.at[j, col, at],
                     s["row_send"].at[j], s["row_recv"].at[j], (chip * 2 + t, to))

    blocks_left = [(i, n, k) for i in range(far) for n in range(2) for k in range(slots)]
    waves, passed = [], []
    flat_lows = lows.reshape(far * cols * 2 * slots, *low.shape[3:])

    def feed(count):
        if not blocks_left[:count]:
            return
        for i, n, k in blocks_left[:count]:
            for e in (1, cols - 1):
                send(low.at[mid + i, n, k], lows.at[i, col, n, k],
                     s["low_send"].at[i], s["wave_recv"].at[len(waves)], (row, (col + e) % cols))
        waves.append(blocks_left[:count])
        del blocks_left[:count]

    def pass_on():
        for wave in range(len(passed), len(waves)):
            passed.append(waves[wave])
            wait_bytes(flat_lows.at[pl.ds(0, 2 * len(waves[wave]))], s["wave_recv"].at[wave])
            for i, n, k in waves[wave]:
                e = 1 if k % 2 == 0 else cols - 1
                block = lows.at[i, (col + cols - e) % cols, n, k]
                send(block, block, s["low_send"].at[i], s["low_recv"].at[i], (row, (col + e) % cols))

    feed_row(0)
    load_idx.wait()
    for e in (2, 1, 3, 0):
        for target in (row, mate):
            if e or target is mate:
                send(idxv.at[core, col], idxv.at[core, col], s["idx_send"], s["idx_recv"],
                     (target, (col + e) % cols))

    @pl.when(at_home)
    def _():
        for j in range(chips):
            for target, half in ((row, core), (mate, 1 - core)):
                at = pl.ds(pl.multiple_of(half * 2 * share, 2 * share), 2 * share)
                for src, dst, k in (
                    (rhs.at[j + 2, place, at], s["rhsc"].at[j], 0),
                    (inv.at[j + 2, place], s["invc"].at[j], 1),
                ):
                    if target is row:
                        pltpu.make_async_copy(src, dst, s["side_recv"].at[j, k]).start()
                    else:
                        send(src, dst, s["side_send"].at[j, k], s["side_recv"].at[j, k], (mate, col))

    feed(FEED[0])
    outv, puts = s["outv"], []

    def put(level, src):
        puts.append(pltpu.make_async_copy(src, out.at[level], s["put_sem"].at[level]))
        puts[-1].start()

    for n in range(2):
        outv[0, n] = rhs0[n, quarter]
    put(0, outv.at[0])
    load_own.wait()
    load_low.wait()
    load_inv.wait()
    load_rhs.wait()

    for level in range(1, depth + 1):
        n_rows = 1 << level
        gather = pairs if level == 1 else s[f"gather{level}"]
        recv = s["gather_recv"].at[level - 1]
        split = is_split(level, mid)
        if level == 1:
            wait_bytes(gather.at[pl.ds(0, 2)], recv)
        elif level <= mid + 1:
            wait_bytes(gather, recv)
        elif split:
            wait_bytes(gather.at[0, pl.ds(0, n_rows // 2 - 1)], recv)
            half = gather.at[core]
            sems = s["mate_send"].at[level - 1], s["mate_recv"].at[level - 1]
            send(half, half, *sems, (mate, col))
        else:
            wait_bytes(gather.at[pl.ds(0, 2 * (n_rows - 1))], recv)
        if level == 1:
            part, got = s["part"], s["got"]
            for n in range(2):
                picked, blocks = [], []
                for k in range(slots):
                    picked.append(gather[idxo[n, k, 0]])
                    blocks.append(lowa[n, k])
                partial = nt_dot(jnp.concatenate(picked, 1), jnp.concatenate(blocks, 1))
                part[:, n] = partial.reshape(cols, share, -1)
            for e in (2, 1, 3):
                to = (col + e) % cols
                send(part.at[to], got.at[e - 1], s["part_send"], s["part_recv"], (row, to))
            for j in range(1, chips):
                feed_row(j)
            feed(FEED[1])
            wait_bytes(idxv.reshape(2 * cols, *idx.shape).at[pl.ds(0, 2 * cols - 1)], s["idx_recv"])
            to_scalar = pltpu.make_async_copy(idxv, idxs, load.at[7])
            to_scalar.start()
            wait_bytes(got, s["part_recv"])
            total = (part[col] + got[0]) + (got[1] + got[2])
        elif level <= mid:
            j = level - 2
            wait_bytes(s["rhsc"].at[j], s["side_recv"].at[j, 0])
            wait_bytes(s["invc"].at[j], s["side_recv"].at[j, 1])
            wait_bytes(lowc.at[j, :, pl.ds(0, slots // 2)], s["pass_recv"].at[j])
            picked, blocks = [], []
            for e in range(cols):
                for k in range(slots):
                    at = idxs[home, e, place, k, level - 1]
                    picked.append(gather[at].reshape(2 * share, -1))
                    blocks.append(lowc[j, e, k])
            total = nt_dot(jnp.concatenate(picked, 1), jnp.concatenate(blocks, 1))
        else:
            i = level - mid - 1
            load_far[i].wait()
            wait_bytes(lows.at[i, 0], s["low_recv"].at[i])
            if split:
                wait_bytes(gather.at[0], s["mate_recv"].at[level - 1])
            sums = []
            for n in range(2):
                picked, blocks = [], []
                for e in range(cols):
                    for k in range(slots):
                        at = idxs[core, e, n, k, level - 1]
                        picked.append(gather[(at >> 1) & 1, at >> 2, at & 1] if split else gather[at])
                        blocks.append(lows[i, e, n, k])
                sums.append(nt_dot(jnp.concatenate(picked, 1), jnp.concatenate(blocks, 1)))
            total = jnp.stack(sums, 0)
        in_row = 1 < level <= mid
        if in_row:
            x = inverse_dot(s["rhsc"][level - 2] - total, s["invc"][level - 2])
            x = [x[q * share : (q + 1) * share] for q in range(2)]
        else:
            x = [inverse_dot(rhsq[level - 1, n] - total[n], invv[level, n]) for n in range(2)]
        if level < depth:
            later = 2 * n_rows
            base, here = row - row % later, row % later
            here_chip = here // 2
            onward = s[f"gather{level + 1}"]
            sems = s["gather_send"].at[level], s["gather_recv"].at[level]
            count = later // 2
            if level <= mid:
                mine = s["held"].at[level - 1]
                for n in range(2):
                    mine[n] = x[n].astype(jnp.bfloat16)
            if level == 1:
                slot = onward.at[pl.ds(here_chip * 4 + core * 2, 2), place]

                def to_chips(d, _):
                    target = base + (here_chip + d) % count * 2 + home
                    for e in (2, 1, 3, 0):
                        send(mine, slot, *sems, (target, (col + e) % cols))
                    return _

                for e in (2, 1, 3):
                    send(mine, slot, *sems, (chip * 2 + home, (col + e) % cols))
                hand(at_home, mine, slot, *sems, (mate, col))
            elif level < mid:
                slot = onward.at[here_chip * 4 + col]

                def to_chips(d, _):
                    target = base + (here_chip + d) % count * 2 + core
                    for e in (2, 1, 3, 0):
                        send(mine, slot, *sems, (target, (col + e) % cols))
                    return _

                for e in (2, 1, 3):
                    send(mine, slot, *sems, (row, (col + e) % cols))
                pltpu.make_async_copy(mine, slot, sems[1]).start()
            elif level == mid:
                slot = onward.at[here_chip * 4 + col]

                def to_chips(d, _):
                    target = base + (here_chip + d) % count * 2
                    for t in range(2):
                        for q in range(2):
                            send(mine.at[q], slot, *sems, (target + t, core * 2 + q))
                    return _

                for q in range(2):
                    to = core * 2 + q
                    send(mine.at[q], slot, *sems, (mate, to))
                    hand(to == col, mine.at[q], slot, *sems, (row, to))
            elif is_split(level + 1, mid):
                mine = onward.at[core, here_chip]

                def to_chips(d, _):
                    send(mine, mine, *sems, (base + (here_chip + d) % count * 2 + core, col))
                    return _

            else:
                mine = onward.at[pl.ds(2 * here, 2)]
                count = later

                def to_chips(d, _):
                    send(mine, mine, *sems, (base + (here + d) % later, col))
                    return _

            if level > mid:
                for n in range(2):
                    mine[n] = x[n].astype(jnp.bfloat16)
            lax.fori_loop(1, count, to_chips, 0)
            if level == 1:
                to_scalar.wait()
            if level < mid:
                j = level - 1
                half = pl.ds(core * (slots // 2), slots // 2)
                wait_bytes(lowc.at[j, :, pl.ds(0, slots // 2)], s["row_recv"].at[j])
                send(lowc.at[j, :, half], lowc.at[j, :, half], s["pass_send"].at[j], s["pass_recv"].at[j],
                     (mate, col))
            feed(sum(i < level + 1 - mid for i, _, _ in blocks_left))
            pass_on()
            feed(FEED[level + 1])
        if in_row:
            j = level - 2
            for q in range(2):
                s["wide"][j, q] = x[q]
                to = core * 2 + q
                hand((to == col) & at_home, s["wide"].at[j, q], s["owned"].at[j, place],
                     s["own_send"].at[j], s["own_recv"].at[j], (chip * 2 + home, to))
        else:
            for n in range(2):
                outv[level, n] = x[n]
            put(level, outv.at[level])
        if level == depth - 1:
            for j in range(chips):
                wait_bytes(s["owned"].at[j], s["own_recv"].at[j])
                put(j + 2, s["owned"].at[j])

    wait_bytes(idxv.reshape(2 * cols, *idx.shape).at[pl.ds(0, 2 * cols - 1)], s["idx_send"])
    wait_bytes(pairs.at[pl.ds(0, 2)], s["gather_send"].at[0])
    wait_bytes(s["got"], s["part_send"])
    for j in range(chips):
        wait_bytes(lowc.at[j, pl.ds(0, cols - 1), pl.ds(0, slots // 2)], s["row_send"].at[j])
        wait_if_away(lowc.at[j, 0, pl.ds(0, slots // 2)], s["row_send"].at[j])
        wait_bytes(lowc.at[j, :, pl.ds(0, slots // 2)], s["pass_send"].at[j])
        wait_bytes(s["wide"].at[j, 0], s["own_send"].at[j])
        wait_if_away(s["wide"].at[j, 0], s["own_send"].at[j])

    @pl.when(at_home)
    def _():
        for j in range(chips):
            wait_bytes(s["rhsc"].at[j], s["side_send"].at[j, 0])
            wait_bytes(s["invc"].at[j], s["side_send"].at[j, 1])

    for level in range(2, depth + 1):
        gather, sent = s[f"gather{level}"], s["gather_send"].at[level - 1]
        n_rows = 1 << level
        if level == 2 or level == mid + 1:
            one = gather.at[pl.ds(0, 2), 0] if level == 2 else gather.at[0]
            rest = gather.at[pl.ds(0, 7)] if level == 2 else gather.at[pl.ds(0, 2 * n_rows - 1)]
            wait_bytes(rest, sent)
            wait_if_away(one, sent)
        elif level <= mid:
            wait_bytes(gather.at[pl.ds(0, 2 * n_rows - 1)], sent)
        elif is_split(level, mid):
            wait_bytes(gather.at[0, pl.ds(0, n_rows // 2 - 1)], sent)
            wait_bytes(gather.at[0], s["mate_send"].at[level - 1])
        else:
            wait_bytes(gather.at[pl.ds(0, 2 * (n_rows - 1))], sent)
    for i in range(far):
        wait_bytes(lows.at[i, pl.ds(0, cols - 1)], s["low_send"].at[i])
    for copy in puts:
        copy.wait()


def is_split(level, mid):
    return level > max(mid + 1, SPLIT_ABOVE)


NAMES = (
    "rhs0", "rhsq", "invv", "lowa", "lows", "lowc", "idxv", "idxs", "idxo", "pairs", "part", "got",
    "rhsc", "invc", "held", "wide", "owned", "load_sem", "own_sem", "idx_send", "idx_recv",
    "gather_send", "gather_recv", "part_send", "part_recv", "low_send", "low_recv", "mate_send",
    "mate_recv", "row_send", "row_recv", "pass_send", "pass_recv", "side_send", "side_recv",
    "own_send", "own_recv", "outv", "put_sem", "wave_recv",
)


def scratch_names(depth):
    return [*NAMES, *(f"gather{level}" for level in range(2, depth + 1))]


def on_device(depth, mid, cols, rhs, inv, low, idx):
    levels, two, wide, block = rhs.shape
    share = wide // cols
    slots = low.shape[2]
    far, chips = depth - mid, mid - 1
    idx = idx.transpose(1, 2, 0)
    dma = pltpu.SemaphoreType.DMA
    f32, bf16 = jnp.float32, jnp.bfloat16
    scratch = [
        pltpu.VMEM((two, wide, block), f32),
        pltpu.VMEM((depth, two, share, block), f32),
        pltpu.VMEM((levels, two, block, block), f32),
        pltpu.VMEM((two, slots, block, block), bf16),
        pltpu.VMEM((far, cols, two, slots, block, block), bf16),
        pltpu.VMEM((chips, cols, slots, block, block), bf16),
        pltpu.VMEM((2, cols, *idx.shape), jnp.int32),
        pltpu.SMEM((2, cols, *idx.shape), jnp.int32),
        pltpu.SMEM(idx.shape, jnp.int32),
        pltpu.VMEM((2 * two, wide, block), bf16),
        pltpu.VMEM((cols, two, share, block), f32),
        pltpu.VMEM((cols - 1, two, share, block), f32),
        pltpu.VMEM((chips, 2 * share, block), f32),
        pltpu.VMEM((chips, block, block), f32),
        pltpu.VMEM((mid, 2, share, block), bf16),
        pltpu.VMEM((chips, 2, share, block), f32),
        pltpu.VMEM((chips, two, share, block), f32),
        dma((8,)), dma((far,)), dma, dma,
        dma((depth,)), dma((depth,)), dma, dma, dma((far,)), dma((far,)), dma((depth,)),
        dma((depth,)), dma((chips,)), dma((chips,)), dma((chips,)), dma((chips,)), dma((chips, 2)), dma((chips, 2)),
        dma((chips,)), dma((chips,)), pltpu.VMEM((levels, two, share, block), f32), dma((levels,)),
        dma((2 * levels,)),
    ]
    for level in range(2, depth + 1):
        rows = two << level
        lead = (rows, 2) if level <= mid else (2, rows // 4, 2) if is_split(level, mid) else (rows,)
        scratch.append(pltpu.VMEM((*lead, share, block), bf16))
    stay = pl.BlockSpec(memory_space=pltpu.HBM)
    return pl.pallas_call(
        functools.partial(kernel, depth, mid, cols),
        out_shape=jax.ShapeDtypeStruct((levels, two, share, block), f32),
        in_specs=[stay] * 4,
        out_specs=stay,
        scratch_shapes=scratch,
        compiler_params=pltpu.CompilerParams(
            collective_id=0, has_side_effects=True, vmem_limit_bytes=61 << 20
        ),
    )(rhs, inv, low, idx)


def solution(mesh):
    depth = mesh.shape["row"].bit_length() - 1
    mid = min(ROW_LEVELS, depth - 1)
    return jax.shard_map(
        functools.partial(on_device, depth, mid, mesh.shape["col"]),
        mesh=mesh,
        in_specs=(
            P(None, "row", None, None),
            P(None, "row", None, None),
            P(None, "row", "col", None, None),
            P(None, "row", "col"),
        ),
        out_specs=P(None, "row", "col", None),
        check_vma=False,
    )
```

```python
import functools

import jax
import jax.numpy as jnp
from jax import lax
from jax.experimental import pallas as pl
from jax.experimental.pallas import tpu as pltpu
from jax.sharding import PartitionSpec as P

MESH = pl.DeviceIdType.MESH
ROW_LEVELS = 3
SPLIT_ABOVE = 4
FEED = (0, 0, 6, 2, 8, 8, 0)


def nt_dot(a, b, precision=None):
    return lax.dot_general(
        a, b, (((1,), (1,)), ((), ())), precision=precision, preferred_element_type=jnp.float32
    )


def two_parts(x):
    high = x.astype(jnp.bfloat16)
    return high, (x - high.astype(jnp.float32)).astype(jnp.bfloat16)


def inverse_dot(resid, inverse):
    (rh, rl), (ih, il) = two_parts(resid), two_parts(inverse)
    return nt_dot(jnp.concatenate([rh, rh, rl], 1), jnp.concatenate([ih, il, ih], 1))


def kernel(depth, mid, cols, rhs, inv, low, idx, out, *scratch):
    s = dict(zip(scratch_names(depth), scratch, strict=True))
    row, col = lax.axis_index("row"), lax.axis_index("col")
    share = rhs.shape[2] // cols
    slots = low.shape[2]
    far, chips = depth - mid, mid - 1
    core, chip = row % 2, row // 2
    mate = row + 1 - 2 * core
    home, place = col // 2, col % 2
    at_home = core == home
    rhs0, rhsq, invv, lowa, lows, lowc, idxv, idxs, idxo, pairs = (
        s[k]
        for k in ("rhs0", "rhsq", "invv", "lowa", "lows", "lowc", "idxv", "idxs", "idxo", "pairs")
    )

    def send(src, dst, send_sem, recv_sem, target):
        pltpu.make_async_remote_copy(
            src_ref=src, dst_ref=dst, send_sem=send_sem, recv_sem=recv_sem,
            device_id=target, device_id_type=MESH,
        ).start()

    def hand(here, src, dst, send_sem, recv_sem, target):
        @pl.when(here)
        def _():
            pltpu.make_async_copy(src, dst, recv_sem).start()

        @pl.when(jnp.logical_not(here))
        def _():
            send(src, dst, send_sem, recv_sem, target)

    def wait_bytes(ref, sem):
        pltpu.make_async_copy(ref, ref, sem).wait()

    def wait_if_away(ref, sem):
        @pl.when(jnp.logical_not(at_home))
        def _():
            wait_bytes(ref, sem)

    load = s["load_sem"]
    quarter = pl.ds(pl.multiple_of(col * share, share), share)
    load_rhs0 = pltpu.make_async_copy(rhs.at[0], rhs0, load.at[0])
    load_inv0 = pltpu.make_async_copy(inv.at[0], invv.at[0], load.at[1])
    load_idx = pltpu.make_async_copy(idx, idxv.at[core, col], load.at[2])
    load_own = pltpu.make_async_copy(idx, idxo, load.at[3])
    load_low = pltpu.make_async_copy(low.at[0], lowa, load.at[4])
    load_inv = pltpu.make_async_copy(
        inv.at[pl.ds(1, depth)], invv.at[pl.ds(1, depth)], load.at[5]
    )
    load_rhs = pltpu.make_async_copy(
        rhs.at[pl.ds(1, depth), :, quarter], rhsq, load.at[6]
    )
    load_far = [
        pltpu.make_async_copy(low.at[mid + i], lows.at[i, col], s["own_sem"].at[i])
        for i in range(far)
    ]
    for copy in (load_rhs0, load_inv0, load_idx, load_own, load_low, load_inv, load_rhs, *load_far):
        copy.start()

    barrier = pltpu.get_barrier_semaphore()
    greeted = 0

    def greet(target):
        pl.semaphore_signal(barrier, 1, device_id=target, device_id_type=MESH)

    for bit in reversed(range(1, depth)):
        n = 2 << bit
        greet((row - row % n + (row % n + n // 2) % n, col))
        greeted += 1
    for e in (2, 1, 3, 0):
        greet((mate, (col + e) % cols))
        greeted += 1
        if e:
            greet((row, (col + e) % cols))
            greeted += 1

    load_rhs0.wait()
    load_inv0.wait()
    for n in range(2):
        x0 = inverse_dot(rhs0[n], invv[0, n])
        pairs[core * 2 + n] = x0.astype(jnp.bfloat16)
        rhs0[n] = x0
    pl.semaphore_wait(barrier, greeted)

    mine = pairs.at[pl.ds(core * 2, 2)]
    send(mine, mine, s["gather_send"].at[0], s["gather_recv"].at[0], (mate, col))

    def feed_row(j):
        for n in range(2):
            to = core * 2 + n
            for t in range(2):
                at = pl.ds(t * (slots // 2), slots // 2)
                hand((to == col) & (core == t), low.at[j + 1, n, at], lowc.at[j, col, at],
                     s["row_send"].at[j], s["row_recv"].at[j], (chip * 2 + t, to))

    blocks_left = [(i, n, k) for i in range(far) for n in range(2) for k in range(slots)]
    waves, passed = [], []
    flat_lows = lows.reshape(far * cols * 2 * slots, *low.shape[3:])

    def feed(count):
        if not blocks_left[:count]:
            return
        for i, n, k in blocks_left[:count]:
            for e in (1, cols - 1):
                send(low.at[mid + i, n, k], lows.at[i, col, n, k],
                     s["low_send"].at[i], s["wave_recv"].at[len(waves)], (row, (col + e) % cols))
        waves.append(blocks_left[:count])
        del blocks_left[:count]

    def pass_on():
        for wave in range(len(passed), len(waves)):
            passed.append(waves[wave])
            wait_bytes(flat_lows.at[pl.ds(0, 2 * len(waves[wave]))], s["wave_recv"].at[wave])
            for i, n, k in waves[wave]:
                e = 1 if k % 2 == 0 else cols - 1
                block = lows.at[i, (col + cols - e) % cols, n, k]
                send(block, block, s["low_send"].at[i], s["low_recv"].at[i], (row, (col + e) % cols))

    feed_row(0)
    load_idx.wait()
    for e in (2, 1, 3, 0):
        for target in (row, mate):
            if e or target is mate:
                send(idxv.at[core, col], idxv.at[core, col], s["idx_send"], s["idx_recv"],
                     (target, (col + e) % cols))

    @pl.when(at_home)
    def _():
        for j in range(chips):
            for target, half in ((row, core), (mate, 1 - core)):
                at = pl.ds(pl.multiple_of(half * 2 * share, 2 * share), 2 * share)
                for src, dst, k in (
                    (rhs.at[j + 2, place, at], s["rhsc"].at[j], 0),
                    (inv.at[j + 2, place], s["invc"].at[j], 1),
                ):
                    if target is row:
                        pltpu.make_async_copy(src, dst, s["side_recv"].at[j, k]).start()
                    else:
                        send(src, dst, s["side_send"].at[j, k], s["side_recv"].at[j, k], (mate, col))

    feed(FEED[0])
    outv, puts = s["outv"], []

    def put(level, src):
        puts.append(pltpu.make_async_copy(src, out.at[level], s["put_sem"].at[level]))
        puts[-1].start()

    for n in range(2):
        outv[0, n] = rhs0[n, quarter]
    put(0, outv.at[0])
    load_own.wait()
    load_low.wait()
    load_inv.wait()
    load_rhs.wait()

    for level in range(1, depth + 1):
        n_rows = 1 << level
        gather = pairs if level == 1 else s[f"gather{level}"]
        recv = s["gather_recv"].at[level - 1]
        split = is_split(level, mid)
        if level == 1:
            wait_bytes(gather.at[pl.ds(0, 2)], recv)
        elif level <= mid + 1:
            wait_bytes(gather, recv)
        elif split:
            wait_bytes(gather.at[0, pl.ds(0, n_rows // 2 - 1)], recv)
            half = gather.at[core]
            sems = s["mate_send"].at[level - 1], s["mate_recv"].at[level - 1]
            send(half, half, *sems, (mate, col))
        else:
            wait_bytes(gather.at[pl.ds(0, 2 * (n_rows - 1))], recv)
        if level == 1:
            part, got = s["part"], s["got"]
            for n in range(2):
                picked, blocks = [], []
                for k in range(slots):
                    picked.append(gather[idxo[n, k, 0]])
                    blocks.append(lowa[n, k])
                partial = nt_dot(jnp.concatenate(picked, 1), jnp.concatenate(blocks, 1))
                part[:, n] = partial.reshape(cols, share, -1)
            for e in (2, 1, 3):
                to = (col + e) % cols
                send(part.at[to], got.at[e - 1], s["part_send"], s["part_recv"], (row, to))
            for j in range(1, chips):
                feed_row(j)
            feed(FEED[1])
            wait_bytes(idxv.reshape(2 * cols, *idx.shape).at[pl.ds(0, 2 * cols - 1)], s["idx_recv"])
            to_scalar = pltpu.make_async_copy(idxv, idxs, load.at[7])
            to_scalar.start()
            wait_bytes(got, s["part_recv"])
            total = (part[col] + got[0]) + (got[1] + got[2])
        elif level <= mid:
            j = level - 2
            wait_bytes(s["rhsc"].at[j], s["side_recv"].at[j, 0])
            wait_bytes(s["invc"].at[j], s["side_recv"].at[j, 1])
            wait_bytes(lowc.at[j, :, pl.ds(0, slots // 2)], s["pass_recv"].at[j])
            picked, blocks = [], []
            for e in range(cols):
                for k in range(slots):
                    at = idxs[home, e, place, k, level - 1]
                    picked.append(gather[at].reshape(2 * share, -1))
                    blocks.append(lowc[j, e, k])
            total = nt_dot(jnp.concatenate(picked, 1), jnp.concatenate(blocks, 1))
        else:
            i = level - mid - 1
            load_far[i].wait()
            wait_bytes(lows.at[i, 0], s["low_recv"].at[i])
            if split:
                wait_bytes(gather.at[0], s["mate_recv"].at[level - 1])
            sums = []
            for n in range(2):
                picked, blocks = [], []
                for e in range(cols):
                    for k in range(slots):
                        at = idxs[core, e, n, k, level - 1]
                        picked.append(gather[(at >> 1) & 1, at >> 2, at & 1] if split else gather[at])
                        blocks.append(lows[i, e, n, k])
                sums.append(nt_dot(jnp.concatenate(picked, 1), jnp.concatenate(blocks, 1)))
            total = jnp.stack(sums, 0)
        in_row = 1 < level <= mid
        if in_row:
            x = inverse_dot(s["rhsc"][level - 2] - total, s["invc"][level - 2])
            x = [x[q * share : (q + 1) * share] for q in range(2)]
        else:
            x = [inverse_dot(rhsq[level - 1, n] - total[n], invv[level, n]) for n in range(2)]
        if level < depth:
            later = 2 * n_rows
            base, here = row - row % later, row % later
            here_chip = here // 2
            onward = s[f"gather{level + 1}"]
            sems = s["gather_send"].at[level], s["gather_recv"].at[level]
            count = later // 2
            if level <= mid:
                mine = s["held"].at[level - 1]
                for n in range(2):
                    mine[n] = x[n].astype(jnp.bfloat16)
            if level == 1:
                slot = onward.at[pl.ds(here_chip * 4 + core * 2, 2), place]

                def to_chips(d, _):
                    target = base + (here_chip + d) % count * 2 + home
                    for e in (2, 1, 3, 0):
                        send(mine, slot, *sems, (target, (col + e) % cols))
                    return _

                for e in (2, 1, 3):
                    send(mine, slot, *sems, (chip * 2 + home, (col + e) % cols))
                hand(at_home, mine, slot, *sems, (mate, col))
            elif level < mid:
                slot = onward.at[here_chip * 4 + col]

                def to_chips(d, _):
                    target = base + (here_chip + d) % count * 2 + core
                    for e in (2, 1, 3, 0):
                        send(mine, slot, *sems, (target, (col + e) % cols))
                    return _

                for e in (2, 1, 3):
                    send(mine, slot, *sems, (row, (col + e) % cols))
                pltpu.make_async_copy(mine, slot, sems[1]).start()
            elif level == mid:
                slot = onward.at[here_chip * 4 + col]

                def to_chips(d, _):
                    target = base + (here_chip + d) % count * 2
                    for t in range(2):
                        for q in range(2):
                            send(mine.at[q], slot, *sems, (target + t, core * 2 + q))
                    return _

                for q in range(2):
                    to = core * 2 + q
                    send(mine.at[q], slot, *sems, (mate, to))
                    hand(to == col, mine.at[q], slot, *sems, (row, to))
            elif is_split(level + 1, mid):
                mine = onward.at[core, here_chip]

                def to_chips(d, _):
                    send(mine, mine, *sems, (base + (here_chip + d) % count * 2 + core, col))
                    return _

            else:
                mine = onward.at[pl.ds(2 * here, 2)]
                count = later

                def to_chips(d, _):
                    send(mine, mine, *sems, (base + (here + d) % later, col))
                    return _

            if level > mid:
                for n in range(2):
                    mine[n] = x[n].astype(jnp.bfloat16)
            lax.fori_loop(1, count, to_chips, 0)
            if level == 1:
                to_scalar.wait()
            if level < mid:
                j = level - 1
                half = pl.ds(core * (slots // 2), slots // 2)
                wait_bytes(lowc.at[j, :, pl.ds(0, slots // 2)], s["row_recv"].at[j])
                send(lowc.at[j, :, half], lowc.at[j, :, half], s["pass_send"].at[j], s["pass_recv"].at[j],
                     (mate, col))
            feed(sum(i < level + 1 - mid for i, _, _ in blocks_left))
            pass_on()
            feed(FEED[level + 1])
        if in_row:
            j = level - 2
            for q in range(2):
                s["wide"][j, q] = x[q]
                to = core * 2 + q
                hand((to == col) & at_home, s["wide"].at[j, q], s["owned"].at[j, place],
                     s["own_send"].at[j], s["own_recv"].at[j], (chip * 2 + home, to))
        else:
            for n in range(2):
                outv[level, n] = x[n]
            put(level, outv.at[level])
        if level == depth - 1:
            for j in range(chips):
                wait_bytes(s["owned"].at[j], s["own_recv"].at[j])
                put(j + 2, s["owned"].at[j])

    wait_bytes(idxv.reshape(2 * cols, *idx.shape).at[pl.ds(0, 2 * cols - 1)], s["idx_send"])
    wait_bytes(pairs.at[pl.ds(0, 2)], s["gather_send"].at[0])
    wait_bytes(s["got"], s["part_send"])
    for j in range(chips):
        wait_bytes(lowc.at[j, pl.ds(0, cols - 1), pl.ds(0, slots // 2)], s["row_send"].at[j])
        wait_if_away(lowc.at[j, 0, pl.ds(0, slots // 2)], s["row_send"].at[j])
        wait_bytes(lowc.at[j, :, pl.ds(0, slots // 2)], s["pass_send"].at[j])
        wait_bytes(s["wide"].at[j, 0], s["own_send"].at[j])
        wait_if_away(s["wide"].at[j, 0], s["own_send"].at[j])

    @pl.when(at_home)
    def _():
        for j in range(chips):
            wait_bytes(s["rhsc"].at[j], s["side_send"].at[j, 0])
            wait_bytes(s["invc"].at[j], s["side_send"].at[j, 1])

    for level in range(2, depth + 1):
        gather, sent = s[f"gather{level}"], s["gather_send"].at[level - 1]
        n_rows = 1 << level
        if level == 2 or level == mid + 1:
            one = gather.at[pl.ds(0, 2), 0] if level == 2 else gather.at[0]
            rest = gather.at[pl.ds(0, 7)] if level == 2 else gather.at[pl.ds(0, 2 * n_rows - 1)]
            wait_bytes(rest, sent)
            wait_if_away(one, sent)
        elif level <= mid:
            wait_bytes(gather.at[pl.ds(0, 2 * n_rows - 1)], sent)
        elif is_split(level, mid):
            wait_bytes(gather.at[0, pl.ds(0, n_rows // 2 - 1)], sent)
            wait_bytes(gather.at[0], s["mate_send"].at[level - 1])
        else:
            wait_bytes(gather.at[pl.ds(0, 2 * (n_rows - 1))], sent)
    for i in range(far):
        wait_bytes(lows.at[i, pl.ds(0, cols - 1)], s["low_send"].at[i])
    for copy in puts:
        copy.wait()


def is_split(level, mid):
    return level > max(mid + 1, SPLIT_ABOVE)


NAMES = (
    "rhs0", "rhsq", "invv", "lowa", "lows", "lowc", "idxv", "idxs", "idxo", "pairs", "part", "got",
    "rhsc", "invc", "held", "wide", "owned", "load_sem", "own_sem", "idx_send", "idx_recv",
    "gather_send", "gather_recv", "part_send", "part_recv", "low_send", "low_recv", "mate_send",
    "mate_recv", "row_send", "row_recv", "pass_send", "pass_recv", "side_send", "side_recv",
    "own_send", "own_recv", "outv", "put_sem", "wave_recv",
)


def scratch_names(depth):
    return [*NAMES, *(f"gather{level}" for level in range(2, depth + 1))]


def on_device(depth, mid, cols, rhs, inv, low, idx):
    levels, two, wide, block = rhs.shape
    share = wide // cols
    slots = low.shape[2]
    far, chips = depth - mid, mid - 1
    idx = idx.transpose(1, 2, 0)
    dma = pltpu.SemaphoreType.DMA
    f32, bf16 = jnp.float32, jnp.bfloat16
    scratch = [
        pltpu.VMEM((two, wide, block), f32),
        pltpu.VMEM((depth, two, share, block), f32),
        pltpu.VMEM((levels, two, block, block), f32),
        pltpu.VMEM((two, slots, block, block), bf16),
        pltpu.VMEM((far, cols, two, slots, block, block), bf16),
        pltpu.VMEM((chips, cols, slots, block, block), bf16),
        pltpu.VMEM((2, cols, *idx.shape), jnp.int32),
        pltpu.SMEM((2, cols, *idx.shape), jnp.int32),
        pltpu.SMEM(idx.shape, jnp.int32),
        pltpu.VMEM((2 * two, wide, block), bf16),
        pltpu.VMEM((cols, two, share, block), f32),
        pltpu.VMEM((cols - 1, two, share, block), f32),
        pltpu.VMEM((chips, 2 * share, block), f32),
        pltpu.VMEM((chips, block, block), f32),
        pltpu.VMEM((mid, 2, share, block), bf16),
        pltpu.VMEM((chips, 2, share, block), f32),
        pltpu.VMEM((chips, two, share, block), f32),
        dma((8,)), dma((far,)), dma, dma,
        dma((depth,)), dma((depth,)), dma, dma, dma((far,)), dma((far,)), dma((depth,)),
        dma((depth,)), dma((chips,)), dma((chips,)), dma((chips,)), dma((chips,)), dma((chips, 2)), dma((chips, 2)),
        dma((chips,)), dma((chips,)), pltpu.VMEM((levels, two, share, block), f32), dma((levels,)),
        dma((2 * levels,)),
    ]
    for level in range(2, depth + 1):
        rows = two << level
        lead = (rows, 2) if level <= mid else (2, rows // 4, 2) if is_split(level, mid) else (rows,)
        scratch.append(pltpu.VMEM((*lead, share, block), bf16))
    stay = pl.BlockSpec(memory_space=pltpu.HBM)
    return pl.pallas_call(
        functools.partial(kernel, depth, mid, cols),
        out_shape=jax.ShapeDtypeStruct((levels, two, share, block), f32),
        in_specs=[stay] * 4,
        out_specs=stay,
        scratch_shapes=scratch,
        compiler_params=pltpu.CompilerParams(
            collective_id=0, has_side_effects=True, vmem_limit_bytes=61 << 20
        ),
    )(rhs, inv, low, idx)


def solution(mesh):
    depth = mesh.shape["row"].bit_length() - 1
    mid = min(ROW_LEVELS, depth - 1)
    return jax.shard_map(
        functools.partial(on_device, depth, mid, mesh.shape["col"]),
        mesh=mesh,
        in_specs=(
            P(None, "row", None, None),
            P(None, "row", None, None),
            P(None, "row", "col", None, None),
            P(None, "row", "col"),
        ),
        out_specs=P(None, "row", "col", None),
        check_vma=False,
    )
```

```python
import functools

import jax
import jax.numpy as jnp
from jax import lax
from jax.experimental import pallas as pl
from jax.experimental.pallas import tpu as pltpu
from jax.sharding import PartitionSpec as P

MESH = pl.DeviceIdType.MESH
ROW_LEVELS = 3
SPLIT_ABOVE = 4
FEED = (0, 0, 7, 1, 8, 8, 0)


def nt_dot(a, b, precision=None):
    return lax.dot_general(
        a, b, (((1,), (1,)), ((), ())), precision=precision, preferred_element_type=jnp.float32
    )


def two_parts(x):
    high = x.astype(jnp.bfloat16)
    return high, (x - high.astype(jnp.float32)).astype(jnp.bfloat16)


def inverse_dot(resid, inverse):
    (rh, rl), (ih, il) = two_parts(resid), two_parts(inverse)
    return nt_dot(jnp.concatenate([rh, rh, rl], 1), jnp.concatenate([ih, il, ih], 1))


def kernel(depth, mid, cols, rhs, inv, low, idx, out, *scratch):
    s = dict(zip(scratch_names(depth), scratch, strict=True))
    row, col = lax.axis_index("row"), lax.axis_index("col")
    share = rhs.shape[2] // cols
    slots = low.shape[2]
    far, chips = depth - mid, mid - 1
    core, chip = row % 2, row // 2
    mate = row + 1 - 2 * core
    home, place = col // 2, col % 2
    at_home = core == home
    rhs0, rhsq, invv, lowa, lows, lowc, idxv, idxs, idxo, pairs = (
        s[k]
        for k in ("rhs0", "rhsq", "invv", "lowa", "lows", "lowc", "idxv", "idxs", "idxo", "pairs")
    )

    def send(src, dst, send_sem, recv_sem, target):
        pltpu.make_async_remote_copy(
            src_ref=src, dst_ref=dst, send_sem=send_sem, recv_sem=recv_sem,
            device_id=target, device_id_type=MESH,
        ).start()

    def hand(here, src, dst, send_sem, recv_sem, target):
        @pl.when(here)
        def _():
            pltpu.make_async_copy(src, dst, recv_sem).start()

        @pl.when(jnp.logical_not(here))
        def _():
            send(src, dst, send_sem, recv_sem, target)

    def wait_bytes(ref, sem):
        pltpu.make_async_copy(ref, ref, sem).wait()

    def wait_if_away(ref, sem):
        @pl.when(jnp.logical_not(at_home))
        def _():
            wait_bytes(ref, sem)

    load = s["load_sem"]
    quarter = pl.ds(pl.multiple_of(col * share, share), share)
    load_rhs0 = pltpu.make_async_copy(rhs.at[0], rhs0, load.at[0])
    load_inv0 = pltpu.make_async_copy(inv.at[0], invv.at[0], load.at[1])
    load_idx = pltpu.make_async_copy(idx, idxv.at[core, col], load.at[2])
    load_own = pltpu.make_async_copy(idx, idxo, load.at[3])
    load_low = pltpu.make_async_copy(low.at[0], lowa, load.at[4])
    load_inv = pltpu.make_async_copy(
        inv.at[pl.ds(1, depth)], invv.at[pl.ds(1, depth)], load.at[5]
    )
    load_rhs = pltpu.make_async_copy(
        rhs.at[pl.ds(1, depth), :, quarter], rhsq, load.at[6]
    )
    load_far = [
        pltpu.make_async_copy(low.at[mid + i], lows.at[i, col], s["own_sem"].at[i])
        for i in range(far)
    ]
    for copy in (load_rhs0, load_inv0, load_idx, load_own, load_low, load_inv, load_rhs, *load_far):
        copy.start()

    barrier = pltpu.get_barrier_semaphore()
    greeted = 0

    def greet(target):
        pl.semaphore_signal(barrier, 1, device_id=target, device_id_type=MESH)

    for bit in reversed(range(1, depth)):
        n = 2 << bit
        greet((row - row % n + (row % n + n // 2) % n, col))
        greeted += 1
    for e in (2, 1, 3, 0):
        greet((mate, (col + e) % cols))
        greeted += 1
        if e:
            greet((row, (col + e) % cols))
            greeted += 1

    load_rhs0.wait()
    load_inv0.wait()
    for n in range(2):
        x0 = inverse_dot(rhs0[n], invv[0, n])
        pairs[core * 2 + n] = x0.astype(jnp.bfloat16)
        rhs0[n] = x0
    pl.semaphore_wait(barrier, greeted)

    mine = pairs.at[pl.ds(core * 2, 2)]
    send(mine, mine, s["gather_send"].at[0], s["gather_recv"].at[0], (mate, col))

    def feed_row(j):
        for n in range(2):
            to = core * 2 + n
            for t in range(2):
                at = pl.ds(t * (slots // 2), slots // 2)
                hand((to == col) & (core == t), low.at[j + 1, n, at], lowc.at[j, col, at],
                     s["row_send"].at[j], s["row_recv"].at[j], (chip * 2 + t, to))

    blocks_left = [(i, n, k) for i in range(far) for n in range(2) for k in range(slots)]
    waves, passed = [], []
    flat_lows = lows.reshape(far * cols * 2 * slots, *low.shape[3:])

    def feed(count):
        if not blocks_left[:count]:
            return
        for i, n, k in blocks_left[:count]:
            for e in (1, cols - 1):
                send(low.at[mid + i, n, k], lows.at[i, col, n, k],
                     s["low_send"].at[i], s["wave_recv"].at[len(waves)], (row, (col + e) % cols))
        waves.append(blocks_left[:count])
        del blocks_left[:count]

    def pass_on():
        for wave in range(len(passed), len(waves)):
            passed.append(waves[wave])
            wait_bytes(flat_lows.at[pl.ds(0, 2 * len(waves[wave]))], s["wave_recv"].at[wave])
            for i, n, k in waves[wave]:
                e = 1 if k % 2 == 0 else cols - 1
                block = lows.at[i, (col + cols - e) % cols, n, k]
                send(block, block, s["low_send"].at[i], s["low_recv"].at[i], (row, (col + e) % cols))

    feed_row(0)
    load_idx.wait()
    for e in (2, 1, 3, 0):
        for target in (row, mate):
            if e or target is mate:
                send(idxv.at[core, col], idxv.at[core, col], s["idx_send"], s["idx_recv"],
                     (target, (col + e) % cols))

    @pl.when(at_home)
    def _():
        for j in range(chips):
            for target, half in ((row, core), (mate, 1 - core)):
                at = pl.ds(pl.multiple_of(half * 2 * share, 2 * share), 2 * share)
                for src, dst, k in (
                    (rhs.at[j + 2, place, at], s["rhsc"].at[j], 0),
                    (inv.at[j + 2, place], s["invc"].at[j], 1),
                ):
                    if target is row:
                        pltpu.make_async_copy(src, dst, s["side_recv"].at[j, k]).start()
                    else:
                        send(src, dst, s["side_send"].at[j, k], s["side_recv"].at[j, k], (mate, col))

    feed(FEED[0])
    outv, puts = s["outv"], []

    def put(level, src):
        puts.append(pltpu.make_async_copy(src, out.at[level], s["put_sem"].at[level]))
        puts[-1].start()

    for n in range(2):
        outv[0, n] = rhs0[n, quarter]
    put(0, outv.at[0])
    load_own.wait()
    load_low.wait()
    load_inv.wait()
    load_rhs.wait()

    for level in range(1, depth + 1):
        n_rows = 1 << level
        gather = pairs if level == 1 else s[f"gather{level}"]
        recv = s["gather_recv"].at[level - 1]
        split = is_split(level, mid)
        if level == 1:
            wait_bytes(gather.at[pl.ds(0, 2)], recv)
        elif level <= mid + 1:
            wait_bytes(gather, recv)
        elif split:
            wait_bytes(gather.at[0, pl.ds(0, n_rows // 2 - 1)], recv)
            half = gather.at[core]
            sems = s["mate_send"].at[level - 1], s["mate_recv"].at[level - 1]
            send(half, half, *sems, (mate, col))
        else:
            wait_bytes(gather.at[pl.ds(0, 2 * (n_rows - 1))], recv)
        if level == 1:
            part, got = s["part"], s["got"]
            for n in range(2):
                picked, blocks = [], []
                for k in range(slots):
                    picked.append(gather[idxo[n, k, 0]])
                    blocks.append(lowa[n, k])
                partial = nt_dot(jnp.concatenate(picked, 1), jnp.concatenate(blocks, 1))
                part[:, n] = partial.reshape(cols, share, -1)
            for e in (2, 1, 3):
                to = (col + e) % cols
                send(part.at[to], got.at[e - 1], s["part_send"], s["part_recv"], (row, to))
            for j in range(1, chips):
                feed_row(j)
            feed(FEED[1])
            wait_bytes(idxv.reshape(2 * cols, *idx.shape).at[pl.ds(0, 2 * cols - 1)], s["idx_recv"])
            to_scalar = pltpu.make_async_copy(idxv, idxs, load.at[7])
            to_scalar.start()
            wait_bytes(got, s["part_recv"])
            total = (part[col] + got[0]) + (got[1] + got[2])
        elif level <= mid:
            j = level - 2
            wait_bytes(s["rhsc"].at[j], s["side_recv"].at[j, 0])
            wait_bytes(s["invc"].at[j], s["side_recv"].at[j, 1])
            wait_bytes(lowc.at[j, :, pl.ds(0, slots // 2)], s["pass_recv"].at[j])
            picked, blocks = [], []
            for e in range(cols):
                for k in range(slots):
                    at = idxs[home, e, place, k, level - 1]
                    picked.append(gather[at].reshape(2 * share, -1))
                    blocks.append(lowc[j, e, k])
            total = nt_dot(jnp.concatenate(picked, 1), jnp.concatenate(blocks, 1))
        else:
            i = level - mid - 1
            load_far[i].wait()
            wait_bytes(lows.at[i, 0], s["low_recv"].at[i])
            if split:
                wait_bytes(gather.at[0], s["mate_recv"].at[level - 1])
            sums = []
            for n in range(2):
                picked, blocks = [], []
                for e in range(cols):
                    for k in range(slots):
                        at = idxs[core, e, n, k, level - 1]
                        picked.append(gather[(at >> 1) & 1, at >> 2, at & 1] if split else gather[at])
                        blocks.append(lows[i, e, n, k])
                sums.append(nt_dot(jnp.concatenate(picked, 1), jnp.concatenate(blocks, 1)))
            total = jnp.stack(sums, 0)
        in_row = 1 < level <= mid
        if in_row:
            x = inverse_dot(s["rhsc"][level - 2] - total, s["invc"][level - 2])
            x = [x[q * share : (q + 1) * share] for q in range(2)]
        else:
            x = [inverse_dot(rhsq[level - 1, n] - total[n], invv[level, n]) for n in range(2)]
        if level < depth:
            later = 2 * n_rows
            base, here = row - row % later, row % later
            here_chip = here // 2
            onward = s[f"gather{level + 1}"]
            sems = s["gather_send"].at[level], s["gather_recv"].at[level]
            count = later // 2
            if level <= mid:
                mine = s["held"].at[level - 1]
                for n in range(2):
                    mine[n] = x[n].astype(jnp.bfloat16)
            if level == 1:
                slot = onward.at[pl.ds(here_chip * 4 + core * 2, 2), place]

                def to_chips(d, _):
                    target = base + (here_chip + d) % count * 2 + home
                    for e in (2, 1, 3, 0):
                        send(mine, slot, *sems, (target, (col + e) % cols))
                    return _

                for e in (2, 1, 3):
                    send(mine, slot, *sems, (chip * 2 + home, (col + e) % cols))
                hand(at_home, mine, slot, *sems, (mate, col))
            elif level < mid:
                slot = onward.at[here_chip * 4 + col]

                def to_chips(d, _):
                    away = count // 2 + d // 2 * (1 - 2 * (d % 2))
                    target = base + (here_chip + away) % count * 2 + core
                    for e in (2, 1, 3, 0):
                        send(mine, slot, *sems, (target, (col + e) % cols))
                    return _

                for e in (2, 1, 3):
                    send(mine, slot, *sems, (row, (col + e) % cols))
                pltpu.make_async_copy(mine, slot, sems[1]).start()
            elif level == mid:
                slot = onward.at[here_chip * 4 + col]

                def to_chips(d, _):
                    away = count // 2 + d // 2 * (1 - 2 * (d % 2))
                    target = base + (here_chip + away) % count * 2
                    for t in range(2):
                        for q in range(2):
                            send(mine.at[q], slot, *sems, (target + t, core * 2 + q))
                    return _

                for q in range(2):
                    to = core * 2 + q
                    send(mine.at[q], slot, *sems, (mate, to))
                    hand(to == col, mine.at[q], slot, *sems, (row, to))
            elif is_split(level + 1, mid):
                mine = onward.at[core, here_chip]

                def to_chips(d, _):
                    away = count // 2 + d // 2 * (1 - 2 * (d % 2))
                    send(mine, mine, *sems, (base + (here_chip + away) % count * 2 + core, col))
                    return _

            else:
                mine = onward.at[pl.ds(2 * here, 2)]
                count = later

                def to_chips(d, _):
                    send(mine, mine, *sems, (base + (here + d) % later, col))
                    return _

            if level > mid:
                for n in range(2):
                    mine[n] = x[n].astype(jnp.bfloat16)
            lax.fori_loop(1, count, to_chips, 0)
            if level == 1:
                to_scalar.wait()
            if level < mid:
                j = level - 1
                half = pl.ds(core * (slots // 2), slots // 2)
                wait_bytes(lowc.at[j, :, pl.ds(0, slots // 2)], s["row_recv"].at[j])
                send(lowc.at[j, :, half], lowc.at[j, :, half], s["pass_send"].at[j], s["pass_recv"].at[j],
                     (mate, col))
            feed(sum(i < level + 1 - mid for i, _, _ in blocks_left))
            pass_on()
            feed(FEED[level + 1])
        if in_row:
            j = level - 2
            for q in range(2):
                s["wide"][j, q] = x[q]
                to = core * 2 + q
                hand((to == col) & at_home, s["wide"].at[j, q], s["owned"].at[j, place],
                     s["own_send"].at[j], s["own_recv"].at[j], (chip * 2 + home, to))
        else:
            for n in range(2):
                outv[level, n] = x[n]
            put(level, outv.at[level])
        if level == depth - 1:
            for j in range(chips):
                wait_bytes(s["owned"].at[j], s["own_recv"].at[j])
                put(j + 2, s["owned"].at[j])

    wait_bytes(idxv.reshape(2 * cols, *idx.shape).at[pl.ds(0, 2 * cols - 1)], s["idx_send"])
    wait_bytes(pairs.at[pl.ds(0, 2)], s["gather_send"].at[0])
    wait_bytes(s["got"], s["part_send"])
    for j in range(chips):
        wait_bytes(lowc.at[j, pl.ds(0, cols - 1), pl.ds(0, slots // 2)], s["row_send"].at[j])
        wait_if_away(lowc.at[j, 0, pl.ds(0, slots // 2)], s["row_send"].at[j])
        wait_bytes(lowc.at[j, :, pl.ds(0, slots // 2)], s["pass_send"].at[j])
        wait_bytes(s["wide"].at[j, 0], s["own_send"].at[j])
        wait_if_away(s["wide"].at[j, 0], s["own_send"].at[j])

    @pl.when(at_home)
    def _():
        for j in range(chips):
            wait_bytes(s["rhsc"].at[j], s["side_send"].at[j, 0])
            wait_bytes(s["invc"].at[j], s["side_send"].at[j, 1])

    for level in range(2, depth + 1):
        gather, sent = s[f"gather{level}"], s["gather_send"].at[level - 1]
        n_rows = 1 << level
        if level == 2 or level == mid + 1:
            one = gather.at[pl.ds(0, 2), 0] if level == 2 else gather.at[0]
            rest = gather.at[pl.ds(0, 7)] if level == 2 else gather.at[pl.ds(0, 2 * n_rows - 1)]
            wait_bytes(rest, sent)
            wait_if_away(one, sent)
        elif level <= mid:
            wait_bytes(gather.at[pl.ds(0, 2 * n_rows - 1)], sent)
        elif is_split(level, mid):
            wait_bytes(gather.at[0, pl.ds(0, n_rows // 2 - 1)], sent)
            wait_bytes(gather.at[0], s["mate_send"].at[level - 1])
        else:
            wait_bytes(gather.at[pl.ds(0, 2 * (n_rows - 1))], sent)
    for i in range(far):
        wait_bytes(lows.at[i, pl.ds(0, cols - 1)], s["low_send"].at[i])
    for copy in puts:
        copy.wait()


def is_split(level, mid):
    return level > max(mid + 1, SPLIT_ABOVE)


NAMES = (
    "rhs0", "rhsq", "invv", "lowa", "lows", "lowc", "idxv", "idxs", "idxo", "pairs", "part", "got",
    "rhsc", "invc", "held", "wide", "owned", "load_sem", "own_sem", "idx_send", "idx_recv",
    "gather_send", "gather_recv", "part_send", "part_recv", "low_send", "low_recv", "mate_send",
    "mate_recv", "row_send", "row_recv", "pass_send", "pass_recv", "side_send", "side_recv",
    "own_send", "own_recv", "outv", "put_sem", "wave_recv",
)


def scratch_names(depth):
    return [*NAMES, *(f"gather{level}" for level in range(2, depth + 1))]


def on_device(depth, mid, cols, rhs, inv, low, idx):
    levels, two, wide, block = rhs.shape
    share = wide // cols
    slots = low.shape[2]
    far, chips = depth - mid, mid - 1
    idx = idx.transpose(1, 2, 0)
    dma = pltpu.SemaphoreType.DMA
    f32, bf16 = jnp.float32, jnp.bfloat16
    scratch = [
        pltpu.VMEM((two, wide, block), f32),
        pltpu.VMEM((depth, two, share, block), f32),
        pltpu.VMEM((levels, two, block, block), f32),
        pltpu.VMEM((two, slots, block, block), bf16),
        pltpu.VMEM((far, cols, two, slots, block, block), bf16),
        pltpu.VMEM((chips, cols, slots, block, block), bf16),
        pltpu.VMEM((2, cols, *idx.shape), jnp.int32),
        pltpu.SMEM((2, cols, *idx.shape), jnp.int32),
        pltpu.SMEM(idx.shape, jnp.int32),
        pltpu.VMEM((2 * two, wide, block), bf16),
        pltpu.VMEM((cols, two, share, block), f32),
        pltpu.VMEM((cols - 1, two, share, block), f32),
        pltpu.VMEM((chips, 2 * share, block), f32),
        pltpu.VMEM((chips, block, block), f32),
        pltpu.VMEM((mid, 2, share, block), bf16),
        pltpu.VMEM((chips, 2, share, block), f32),
        pltpu.VMEM((chips, two, share, block), f32),
        dma((8,)), dma((far,)), dma, dma,
        dma((depth,)), dma((depth,)), dma, dma, dma((far,)), dma((far,)), dma((depth,)),
        dma((depth,)), dma((chips,)), dma((chips,)), dma((chips,)), dma((chips,)), dma((chips, 2)), dma((chips, 2)),
        dma((chips,)), dma((chips,)), pltpu.VMEM((levels, two, share, block), f32), dma((levels,)),
        dma((2 * levels,)),
    ]
    for level in range(2, depth + 1):
        rows = two << level
        lead = (rows, 2) if level <= mid else (2, rows // 4, 2) if is_split(level, mid) else (rows,)
        scratch.append(pltpu.VMEM((*lead, share, block), bf16))
    stay = pl.BlockSpec(memory_space=pltpu.HBM)
    return pl.pallas_call(
        functools.partial(kernel, depth, mid, cols),
        out_shape=jax.ShapeDtypeStruct((levels, two, share, block), f32),
        in_specs=[stay] * 4,
        out_specs=stay,
        scratch_shapes=scratch,
        compiler_params=pltpu.CompilerParams(
            collective_id=0, has_side_effects=True, vmem_limit_bytes=61 << 20
        ),
    )(rhs, inv, low, idx)


def solution(mesh):
    depth = mesh.shape["row"].bit_length() - 1
    mid = min(ROW_LEVELS, depth - 1)
    return jax.shard_map(
        functools.partial(on_device, depth, mid, mesh.shape["col"]),
        mesh=mesh,
        in_specs=(
            P(None, "row", None, None),
            P(None, "row", None, None),
            P(None, "row", "col", None, None),
            P(None, "row", "col"),
        ),
        out_specs=P(None, "row", "col", None),
        check_vma=False,
    )
```
